32 devices in a mesh: group: 2 (over y), col: 4 (over z), row: 2 (over x), section: 2 (over core).
Axes of the slice: x: 2, y: 2, z: 4, core: 2. Of those that a mesh axis runs over, the one named last changes fastest.
Arguments:
- tokens: bfloat16 [2, 256, 8192], P(None, ('group', 'col'), 'row'), parts along dimension 1, may hold values from -12 to 12, as said below
- norm_gain: float32 [2, 8192], P('section', 'row'), may hold values from 0.5 to 1.5
- w_gate: bfloat16 [2, 8192, 14336], P('section', 'row', 'col'), may hold values from -0.0625 to 0.0625
- w_up: bfloat16 [2, 8192, 14336], P('section', 'row', 'col'), may hold values from -0.0625 to 0.0625
- w_down: bfloat16 [2, 14336, 8192], P('section', 'col', 'row'), may hold values from -0.046875 to 0.046875
Outputs:
- block_out: bfloat16 [2, 2, 256, 8192], P('section', None, ('group', 'col'), 'row'), parts along dimension 2
The draws below stay inside these ranges and needn't reach their ends.
There are 2 independent parts, one for each index of `group`. The reference program is written for one: setup_inputs(seed, part) draws one part's arguments, and reference() takes and returns one part's arrays. A program takes and returns all parts, laid end to end along the dimension named above; an argument that names none is the same for every part. Nothing has to cross between parts.
Inputs may be any that keep to these rules, and one draw needn't show every extreme that they name: `tokens`: dense real activations.
All inputs are finite; a program needn't handle non-finite values.
Results may differ from the reference program's by a relative error of at most 0.024.
Values may be sent and summed in bfloat16 or wider, within the bound.
A program may use at most 128 MiB of HBM per device.

```python
import jax
import jax.numpy as jnp
from jax import lax

D = 8192
FF = 14336
MB = 2
TOK = 128
LAYERS = 2
N_COL = 4
N_ROW = 2


def draw_tokens(key, part):
    first_key, second_key = jax.random.split(jax.random.fold_in(key, 11))
    position = jnp.arange(D, dtype=jnp.float32) / D
    columns = 0.4 * jnp.exp(jnp.log(3.0) * position)
    rows = 0.5 * jnp.exp(jnp.log(3.0) * jax.random.uniform(second_key, (MB, TOK, 1), jnp.float32))
    values = jnp.clip(jax.random.normal(first_key, (MB, TOK, D), jnp.float32), -6.0, 6.0)
    return (values * columns[None, None, :] * rows).astype(jnp.bfloat16)


def block_scale(rng, shape, cuts, smallest, top_value):
    level = 1.0
    for dim, shards_of in cuts:
        steps = jax.random.uniform(jax.random.fold_in(jax.random.fold_in(rng, 6), dim), (shards_of,), jnp.float32, smallest / len(cuts), top_value / len(cuts))
        level = level * jnp.repeat(jnp.exp(steps), shape[dim] // shards_of).reshape((-1,) + (1,) * (len(shape) - 1 - dim))
    return level


def bell_draw(key, shape, width, bound, cuts=(), kind=jnp.bfloat16):
    level = block_scale(key, shape, cuts, -0.22, 0.18) if cuts else 1.0
    drawn = jax.random.normal(key, shape, jnp.float32) * width * level
    return jnp.minimum(jnp.maximum(drawn, -bound), bound).astype(kind)


def setup_inputs(seed: int = 0, part: int = 0) -> dict:
    keys = jax.random.split(jax.random.key(seed), 6)
    part_splits = jax.random.split(jax.random.fold_in(keys[5], part), 6)
    return {
        "tokens": draw_tokens(jax.random.fold_in(jax.random.fold_in(keys[5], part), 71), part),
        "norm_gain": jnp.clip(0.5 + 1.0 * jax.random.uniform(keys[1], (LAYERS, D), jnp.float32) ** block_scale(keys[1], (LAYERS, D), ((0, 2), (1, 2)), -0.2, 0.2), 0.5, 1.5),
        "w_gate": bell_draw(keys[2], (LAYERS, D, FF), D ** -0.5, 0.0625, ((0, 2), (1, 2), (2, 4))),
        "w_up": bell_draw(keys[3], (LAYERS, D, FF), D ** -0.5, 0.0625, ((0, 2), (1, 2), (2, 4))),
        "w_down": bell_draw(keys[4], (LAYERS, FF, D), FF ** -0.5, 0.046875, ((0, 2), (1, 4), (2, 2))),
    }


EPS = 1e-05

def rounded(value):
    return lax.optimization_barrier(value.astype(jnp.bfloat16)).astype(jnp.float32)

def one_block(h_in, gain, w_gate, w_up, w_down):
    wide = h_in.astype(jnp.float32)
    mean_sq = lax.optimization_barrier(jnp.mean(wide * wide, axis=1, keepdims=True))
    normed = (wide * lax.rsqrt(mean_sq + EPS) * gain[None, :]).astype(jnp.bfloat16)
    row_block = D // N_ROW
    gate = jnp.zeros((h_in.shape[0], FF), jnp.float32)
    up = jnp.zeros((h_in.shape[0], FF), jnp.float32)
    for index in range(N_ROW):
        piece = normed[:, index * row_block:(index + 1) * row_block]
        gate = gate + rounded(jnp.dot(piece, w_gate[index * row_block:(index + 1) * row_block], preferred_element_type=jnp.float32))
        up = up + rounded(jnp.dot(piece, w_up[index * row_block:(index + 1) * row_block], preferred_element_type=jnp.float32))
    hidden = (jax.nn.silu(gate) * up).astype(jnp.bfloat16)
    col_block = FF // N_COL
    ffn = jnp.zeros((h_in.shape[0], D), jnp.float32)
    for index in range(N_COL):
        piece = hidden[:, index * col_block:(index + 1) * col_block]
        ffn = ffn + rounded(jnp.dot(piece, w_down[index * col_block:(index + 1) * col_block], preferred_element_type=jnp.float32))
    return (wide + ffn).astype(jnp.bfloat16)

def reference(tokens, norm_gain, w_gate, w_up, w_down):
    layers_out = []
    current = [tokens[m] for m in range(MB)]
    for layer in range(LAYERS):
        current = [one_block(current[m], norm_gain[layer], w_gate[layer], w_up[layer], w_down[layer]) for m in range(MB)]
        layers_out.append(jnp.stack(current, axis=0))
    return jnp.stack(layers_out, axis=0)
```

```python
import functools

import jax
import jax.numpy as jnp
from jax import lax
from jax.experimental import pallas as pl
from jax.experimental.pallas import tpu as pltpu
from jax.sharding import PartitionSpec as P

EPS = 1e-05
LAG = 3
VMEM_BYTES = 67_043_328
RESERVE = 3 * 1024 * 1024
MESH = pl.DeviceIdType.MESH


def widest(size, options):
    return next(w for w in options if size % w == 0)


def kernel(
    dims,
    tok_ref, gain_ref, wg_ref, wu_ref, wd_ref, out_ref,
    wa, wb, hbuf, ss, sr, xb, gu, gr, hid, fo, fr,
    wa_sem, wb_sem, h_send, h_recv, ss_send, ss_recv, ag_send, ag_recv,
    gu_send, gu_recv, hd_send, hd_recv, fo_send, fo_recv,
):
    C, R, M, TC, DR, FC, D, F, n, S, N, nb, SB = dims
    T = TC * C
    TS = T // R
    c = lax.axis_index("col")
    r = lax.axis_index("row")
    s = lax.axis_index("section")

    def load_a(q):
        slot = lax.rem(q, S)
        cols = pl.ds(pl.multiple_of(lax.rem(q, n) * F, F), F)
        return (
            pltpu.make_async_copy(wg_ref.at[0, :, cols], wa.at[slot, 0], wa_sem.at[slot, 0]),
            pltpu.make_async_copy(wu_ref.at[0, :, cols], wa.at[slot, 1], wa_sem.at[slot, 1]),
        )

    def load_b(q):
        slot = lax.rem(q, SB)
        cols = pl.ds(pl.multiple_of(lax.rem(q, nb) * N, N), N)
        return pltpu.make_async_copy(wd_ref.at[0, :, cols], wb.at[slot], wb_sem.at[slot])

    def col_peer(d):
        return lax.rem(c + d, C)

    def row_peer(d):
        return lax.rem(r + d, R)

    def tok_rows(index):
        return pl.ds(pl.multiple_of(index * TC, TC), TC)

    def share_rows(index):
        return pl.ds(pl.multiple_of(index * TS, TS), TS)

    def ss_copy(m, d):
        return pltpu.make_async_remote_copy(
            src_ref=ss.at[m], dst_ref=sr.at[m, d - 1],
            send_sem=ss_send.at[m, d - 1], recv_sem=ss_recv.at[m, d - 1],
            device_id={"row": row_peer(d)}, device_id_type=MESH)

    def ag_copy(m, d, owner):
        return pltpu.make_async_remote_copy(
            src_ref=xb.at[m, tok_rows(owner)], dst_ref=xb.at[m, tok_rows(owner)],
            send_sem=ag_send.at[m, d - 1], recv_sem=ag_recv.at[m, d - 1],
            device_id={"col": col_peer(d)}, device_id_type=MESH)

    def gu_copy(m, i, d):
        return pltpu.make_async_remote_copy(
            src_ref=gu.at[m, i, share_rows(row_peer(d))], dst_ref=gr.at[m, i, d - 1],
            send_sem=gu_send.at[m, i, d - 1], recv_sem=gu_recv.at[m, i, d - 1],
            device_id={"row": row_peer(d)}, device_id_type=MESH)

    def hd_copy(m, i, d, owner):
        k = lax.rem(m * (n - S) + i, n)
        cols = pl.ds(pl.multiple_of(k * F, F), F)
        return pltpu.make_async_remote_copy(
            src_ref=hid.at[m, share_rows(owner), cols], dst_ref=hid.at[m, share_rows(owner), cols],
            send_sem=hd_send.at[m, i, d - 1], recv_sem=hd_recv.at[m, i, d - 1],
            device_id={"row": row_peer(d)}, device_id_type=MESH)

    def fo_copy(m, i, d):
        v = lax.rem(m * (nb - SB) + i, nb)
        cols = pl.ds(pl.multiple_of(v * N, N), N)
        return pltpu.make_async_remote_copy(
            src_ref=fo.at[m, tok_rows(col_peer(d)), cols], dst_ref=fr.at[m, d - 1, :, cols],
            send_sem=fo_send.at[m, i, d - 1], recv_sem=fo_recv.at[m, i, d - 1],
            device_id={"col": col_peer(d)}, device_id_type=MESH)

    def h_copy(m):
        return pltpu.make_async_remote_copy(
            src_ref=out_ref.at[0, m], dst_ref=hbuf.at[m],
            send_sem=h_send.at[m], recv_sem=h_recv.at[m],
            device_id={"section": 1 - s}, device_id_type=MESH)

    for q in range(S):
        for copy in load_a(q):
            copy.start()
    for q in range(SB):
        load_b(q).start()

    barrier = pltpu.get_barrier_semaphore()
    for d in range(1, C):
        pl.semaphore_signal(barrier, inc=1, device_id={"col": col_peer(d)}, device_id_type=MESH)
    for d in range(1, R):
        pl.semaphore_signal(barrier, inc=1, device_id={"row": row_peer(d)}, device_id_type=MESH)
    pl.semaphore_signal(barrier, inc=1, device_id={"section": 1 - s}, device_id_type=MESH)
    pl.semaphore_wait(barrier, C + R - 1)

    for m in range(M):
        @pl.when(s == 0)
        def _():
            hbuf[m] = tok_ref[m]

        @pl.when(s == 1)
        def _():
            h_copy(m).wait_recv()

        wide = hbuf[m].astype(jnp.float32)
        ss[m] = jnp.broadcast_to(jnp.sum(wide * wide, axis=1, keepdims=True), (TC, 128))
        for d in range(1, R):
            ss_copy(m, d).start()
        total = ss[m]
        for d in range(1, R):
            ss_copy(m, d).wait_recv()
            total = total + sr[m, d - 1]
        scale = lax.rsqrt(total[:, :1] / D + EPS)
        normed = hbuf[m].astype(jnp.float32) * scale * gain_ref[...]
        xb[m, tok_rows(c)] = normed.astype(jnp.bfloat16)
        for d in range(1, C):
            ag_copy(m, d, c).start()

    def up_step(t, carry):
        @pl.when(t < M * n)
        def _():
            m = lax.div(t, n)
            i = lax.rem(t, n)
            q = m * (n - S) + i
            slot = lax.rem(q, S)

            @pl.when(i == 0)
            def _():
                for d in range(1, C):
                    ag_copy(m, d, lax.rem(c + C - d, C)).wait_recv()

            @pl.when(jnp.logical_or(m == 0, i >= S))
            def _():
                for copy in load_a(q):
                    copy.wait()

            x = xb[m]
            for part in range(2):
                gu[m, i, :, part * F:(part + 1) * F] = jnp.dot(
                    x, wa[slot, part], preferred_element_type=jnp.float32
                ).astype(jnp.bfloat16)
            for d in range(1, R):
                gu_copy(m, i, d).start()

            @pl.when(i < n - S)
            def _():
                for copy in load_a(q + S):
                    copy.start()

        @pl.when(t >= LAG)
        def _():
            e = t - LAG
            m = lax.div(e, n)
            i = lax.rem(e, n)
            pair = gu[m, i, share_rows(r)].astype(jnp.float32)
            for d in range(1, R):
                gu_copy(m, i, d).wait_recv()
                pair = pair + gr[m, i, d - 1].astype(jnp.float32)
            gate = pair[:, :F]
            act = gate / (1.0 + jnp.exp(-gate)) * pair[:, F:]
            k = lax.rem(m * (n - S) + i, n)
            cols = pl.ds(pl.multiple_of(k * F, F), F)
            hid[m, share_rows(r), cols] = act.astype(jnp.bfloat16)
            for d in range(1, R):
                hd_copy(m, i, d, r).start()

        return carry

    lax.fori_loop(0, M * n + LAG, up_step, 0)

    def down_step(t, carry):
        m = lax.div(t, nb)
        i = lax.rem(t, nb)
        q = m * (nb - SB) + i
        slot = lax.rem(q, SB)

        @pl.when(i == 0)
        def _():
            def wait_hidden(j, inner):
                for d in range(1, R):
                    hd_copy(m, j, d, lax.rem(r + R - d, R)).wait_recv()
                return inner

            lax.fori_loop(0, n, wait_hidden, 0)

        @pl.when(jnp.logical_or(m == 0, i >= SB))
        def _():
            load_b(q).wait()

        cols = pl.ds(pl.multiple_of(lax.rem(q, nb) * N, N), N)
        fo[m, :, cols] = jnp.dot(
            hid[m], wb[slot], preferred_element_type=jnp.float32
        ).astype(jnp.bfloat16)
        for d in range(1, C):
            fo_copy(m, i, d).start()

        @pl.when(i < nb - SB)
        def _():
            load_b(q + SB).start()

        return carry

    lax.fori_loop(0, M * nb, down_step, 0)

    for m in range(M):
        def finish(i, carry):
            v = lax.rem(m * (nb - SB) + i, nb)
            cols = pl.ds(pl.multiple_of(v * N, N), N)
            ffn = fo[m, tok_rows(c), cols].astype(jnp.float32)
            for d in range(1, C):
                fo_copy(m, i, d).wait_recv()
                ffn = ffn + fr[m, d - 1, :, cols].astype(jnp.float32)
            out_ref[0, m, :, cols] = (hbuf[m, :, cols].astype(jnp.float32) + ffn).astype(jnp.bfloat16)
            return carry

        lax.fori_loop(0, nb, finish, 0)

        @pl.when(s == 0)
        def _():
            h_copy(m).start()

    for m in range(M):
        @pl.when(s == 0)
        def _():
            h_copy(m).wait_send()

        for d in range(1, R):
            ss_copy(m, d).wait_send()
        for d in range(1, C):
            ag_copy(m, d, c).wait_send()

        def drain_row(i, carry):
            for d in range(1, R):
                gu_copy(m, i, d).wait_send()
                hd_copy(m, i, d, r).wait_send()
            return carry

        lax.fori_loop(0, n, drain_row, 0)

        def drain_col(i, carry):
            for d in range(1, C):
                fo_copy(m, i, d).wait_send()
            return carry

        lax.fori_loop(0, nb, drain_col, 0)


def on_device(tokens, norm_gain, w_gate, w_up, w_down):
    C = lax.axis_size("col")
    R = lax.axis_size("row")
    M, TC, DR = tokens.shape
    FC = w_gate.shape[2]
    D = DR * R
    T = TC * C
    TS = T // R
    F = widest(FC, (256, 128))
    n = FC // F
    N = widest(DR, (512, 256, 128))
    nb = DR // N
    bf, f32 = jnp.bfloat16, jnp.float32
    acts = [
        ((M, TC, DR), bf),
        ((M, TC, 128), f32),
        ((M, R - 1, TC, 128), f32),
        ((M, T, DR), bf),
        ((M, n, T, 2 * F), bf),
        ((M, n, R - 1, TS, 2 * F), bf),
        ((M, T, FC), bf),
        ((M, T, DR), bf),
        ((M, C - 1, TC, DR), bf),
    ]

    def size(shape, dtype):
        total = jnp.dtype(dtype).itemsize
        for extent in shape:
            total *= extent
        return total

    used = sum(size(*a) for a in acts) + 2 * size((M, TC, DR), bf) + 8 * size((1, DR), f32)
    room = VMEM_BYTES - RESERVE - used
    a_bytes = size((2, DR, F), bf)
    b_bytes = size((FC, N), bf)
    SB = min(nb, max(2, (room // 3) // b_bytes))
    S = min(n, (room - SB * b_bytes) // a_bytes)
    dma = pltpu.SemaphoreType.DMA
    dims = (C, R, M, TC, DR, FC, D, F, n, S, N, nb, SB)
    vmem = pl.BlockSpec(memory_space=pltpu.VMEM)
    hbm = pl.BlockSpec(memory_space=pl.ANY)
    return pl.pallas_call(
        functools.partial(kernel, dims),
        out_shape=jax.ShapeDtypeStruct((1, M, TC, DR), bf),
        in_specs=[vmem, vmem, hbm, hbm, hbm],
        out_specs=vmem,
        scratch_shapes=[
            pltpu.VMEM((S, 2, DR, F), bf),
            pltpu.VMEM((SB, FC, N), bf),
            *[pltpu.VMEM(shape, dtype) for shape, dtype in acts],
            dma((S, 2)), dma((SB,)),
            dma((M,)), dma((M,)),
            dma((M, R - 1)), dma((M, R - 1)),
            dma((M, C - 1)), dma((M, C - 1)),
            dma((M, n, R - 1)), dma((M, n, R - 1)),
            dma((M, n, R - 1)), dma((M, n, R - 1)),
            dma((M, nb, C - 1)), dma((M, nb, C - 1)),
        ],
        compiler_params=pltpu.CompilerParams(
            collective_id=0, has_side_effects=True, vmem_limit_bytes=VMEM_BYTES
        ),
        name="two_blocks",
    )(tokens, norm_gain, w_gate, w_up, w_down)


def solution(mesh):
    placed = (
        P(None, ("group", "col"), "row"),
        P("section", "row"),
        P("section", "row", "col"),
        P("section", "row", "col"),
        P("section", "col", "row"),
    )
    return jax.shard_map(
        on_device,
        mesh=mesh,
        in_specs=placed,
        out_specs=P("section", None, ("group", "col"), "row"),
        check_vma=False,
    )
```

```python
import functools

import jax
import jax.numpy as jnp
from jax import lax
from jax.experimental import pallas as pl
from jax.experimental.pallas import tpu as pltpu
from jax.sharding import PartitionSpec as P

EPS = 1e-05
LAG = 3
LATE = 5
VMEM_BYTES = 67_043_328
RESERVE = 3 * 1024 * 1024
MESH = pl.DeviceIdType.MESH


def widest(size, options):
    return next(w for w in options if size % w == 0)


def kernel(
    dims,
    tok_ref, gain_ref, wg_ref, wu_ref, wd_ref, out_ref,
    wa, wb, hbuf, ss, sr, xb, gu, gr, hid, fo, fr,
    wa_sem, wb_sem, h_send, h_recv, ss_send, ss_recv, ag_send, ag_recv,
    gu_send, gu_recv, hd_send, hd_recv, fo_send, fo_recv,
):
    C, R, M, TC, DR, FC, D, F, n, S, N, nb, SB = dims
    T = TC * C
    TS = T // R
    CLOSE = min(LATE, n + LAG - 1)
    c = lax.axis_index("col")
    r = lax.axis_index("row")
    s = lax.axis_index("section")

    def load_a(q):
        slot = lax.rem(q, S)
        cols = pl.ds(pl.multiple_of(lax.rem(q, n) * F, F), F)
        return (
            pltpu.make_async_copy(wg_ref.at[0, :, cols], wa.at[slot, 0], wa_sem.at[slot, 0]),
            pltpu.make_async_copy(wu_ref.at[0, :, cols], wa.at[slot, 1], wa_sem.at[slot, 1]),
        )

    def load_b(q):
        slot = lax.rem(q, SB)
        cols = pl.ds(pl.multiple_of(lax.rem(q, nb) * N, N), N)
        return pltpu.make_async_copy(wd_ref.at[0, :, cols], wb.at[slot], wb_sem.at[slot])

    def col_peer(d):
        return lax.rem(c + d, C)

    def row_peer(d):
        return lax.rem(r + d, R)

    def tok_rows(index):
        return pl.ds(pl.multiple_of(index * TC, TC), TC)

    def share_rows(index):
        return pl.ds(pl.multiple_of(index * TS, TS), TS)

    def ss_copy(m, d):
        return pltpu.make_async_remote_copy(
            src_ref=ss.at[m], dst_ref=sr.at[m, d - 1],
            send_sem=ss_send.at[m, d - 1], recv_sem=ss_recv.at[m, d - 1],
            device_id={"row": row_peer(d)}, device_id_type=MESH)

    def ag_copy(m, d, owner):
        return pltpu.make_async_remote_copy(
            src_ref=xb.at[m, tok_rows(owner)], dst_ref=xb.at[m, tok_rows(owner)],
            send_sem=ag_send.at[m, d - 1], recv_sem=ag_recv.at[m, d - 1],
            device_id={"col": col_peer(d)}, device_id_type=MESH)

    def gu_copy(m, i, d):
        return pltpu.make_async_remote_copy(
            src_ref=gu.at[m, i, share_rows(row_peer(d))], dst_ref=gr.at[m, i, d - 1],
            send_sem=gu_send.at[m, i, d - 1], recv_sem=gu_recv.at[m, i, d - 1],
            device_id={"row": row_peer(d)}, device_id_type=MESH)

    def hd_copy(m, i, d, owner):
        k = lax.rem(m * (n - S) + i, n)
        cols = pl.ds(pl.multiple_of(k * F, F), F)
        return pltpu.make_async_remote_copy(
            src_ref=hid.at[m, share_rows(owner), cols], dst_ref=hid.at[m, share_rows(owner), cols],
            send_sem=hd_send.at[m, i, d - 1], recv_sem=hd_recv.at[m, i, d - 1],
            device_id={"row": row_peer(d)}, device_id_type=MESH)

    def fo_copy(m, i, d):
        v = lax.rem(m * (nb - SB) + i, nb)
        cols = pl.ds(pl.multiple_of(v * N, N), N)
        return pltpu.make_async_remote_copy(
            src_ref=fo.at[m, tok_rows(col_peer(d)), cols], dst_ref=fr.at[m, d - 1, :, cols],
            send_sem=fo_send.at[m, i, d - 1], recv_sem=fo_recv.at[m, i, d - 1],
            device_id={"col": col_peer(d)}, device_id_type=MESH)

    def h_copy(m):
        return pltpu.make_async_remote_copy(
            src_ref=out_ref.at[0, m], dst_ref=hbuf.at[m],
            send_sem=h_send.at[m], recv_sem=h_recv.at[m],
            device_id={"section": 1 - s}, device_id_type=MESH)

    for q in range(S):
        for copy in load_a(q):
            copy.start()
    for q in range(SB):
        load_b(q).start()

    barrier = pltpu.get_barrier_semaphore()
    for d in range(1, C):
        pl.semaphore_signal(barrier, inc=1, device_id={"col": col_peer(d)}, device_id_type=MESH)
    for d in range(1, R):
        pl.semaphore_signal(barrier, inc=1, device_id={"row": row_peer(d)}, device_id_type=MESH)
    pl.semaphore_signal(barrier, inc=1, device_id={"section": 1 - s}, device_id_type=MESH)
    pl.semaphore_wait(barrier, C + R - 1)

    def norm(m):
        @pl.when(s == 0)
        def _():
            hbuf[m] = tok_ref[m]

        @pl.when(s == 1)
        def _():
            h_copy(m).wait_recv()

        wide = hbuf[m].astype(jnp.float32)
        ss[m] = jnp.broadcast_to(jnp.sum(wide * wide, axis=1, keepdims=True), (TC, 128))
        for d in range(1, R):
            ss_copy(m, d).start()
        total = ss[m]
        for d in range(1, R):
            ss_copy(m, d).wait_recv()
            total = total + sr[m, d - 1]
        scale = lax.rsqrt(total[:, :1] / D + EPS)
        normed = hbuf[m].astype(jnp.float32) * scale * gain_ref[...]
        xb[m, tok_rows(c)] = normed.astype(jnp.bfloat16)
        for d in range(1, C):
            ag_copy(m, d, c).start()

    def close(m):
        def finish(i, carry):
            v = lax.rem(m * (nb - SB) + i, nb)
            cols = pl.ds(pl.multiple_of(v * N, N), N)
            ffn = fo[m, tok_rows(c), cols].astype(jnp.float32)
            for d in range(1, C):
                fo_copy(m, i, d).wait_recv()
                ffn = ffn + fr[m, d - 1, :, cols].astype(jnp.float32)
            out_ref[0, m, :, cols] = (hbuf[m, :, cols].astype(jnp.float32) + ffn).astype(jnp.bfloat16)
            return carry

        lax.fori_loop(0, nb, finish, 0)

        @pl.when(s == 0)
        def _():
            h_copy(m).start()

    def up_step(m, t, carry):
        @pl.when(t < n)
        def _():
            i = t
            q = m * (n - S) + i
            slot = lax.rem(q, S)

            @pl.when(i == 0)
            def _():
                for d in range(1, C):
                    ag_copy(m, d, lax.rem(c + C - d, C)).wait_recv()

            @pl.when(i >= 0 if m == 0 else i >= S)
            def _():
                for copy in load_a(q):
                    copy.wait()

            x = xb[m]
            for part in range(2):
                gu[m, i, :, part * F:(part + 1) * F] = jnp.dot(
                    x, wa[slot, part], preferred_element_type=jnp.float32
                ).astype(jnp.bfloat16)
            for d in range(1, R):
                gu_copy(m, i, d).start()

            @pl.when(i < n - S)
            def _():
                for copy in load_a(q + S):
                    copy.start()

        @pl.when(t >= LAG)
        def _():
            i = t - LAG
            pair = gu[m, i, share_rows(r)].astype(jnp.float32)
            for d in range(1, R):
                gu_copy(m, i, d).wait_recv()
                pair = pair + gr[m, i, d - 1].astype(jnp.float32)
            gate = pair[:, :F]
            act = gate / (1.0 + jnp.exp(-gate)) * pair[:, F:]
            k = lax.rem(m * (n - S) + i, n)
            cols = pl.ds(pl.multiple_of(k * F, F), F)
            hid[m, share_rows(r), cols] = act.astype(jnp.bfloat16)
            for d in range(1, R):
                hd_copy(m, i, d, r).start()

        if m > 0:
            @pl.when(t == CLOSE)
            def _():
                close(m - 1)

        return carry

    def down_step(m, i, carry):
        q = m * (nb - SB) + i
        slot = lax.rem(q, SB)

        @pl.when(i == 0)
        def _():
            def wait_hidden(j, inner):
                for d in range(1, R):
                    hd_copy(m, j, d, lax.rem(r + R - d, R)).wait_recv()
                return inner

            lax.fori_loop(0, n, wait_hidden, 0)

        @pl.when(i >= 0 if m == 0 else i >= SB)
        def _():
            load_b(q).wait()

        cols = pl.ds(pl.multiple_of(lax.rem(q, nb) * N, N), N)
        fo[m, :, cols] = jnp.dot(
            hid[m], wb[slot], preferred_element_type=jnp.float32
        ).astype(jnp.bfloat16)
        for d in range(1, C):
            fo_copy(m, i, d).start()

        @pl.when(i < nb - SB)
        def _():
            load_b(q + SB).start()

        return carry


    for m in range(M):
        if m == 0:
            norm(0)

            @pl.when(s == 0)
            def _():
                for later in range(1, M):
                    norm(later)
        else:
            @pl.when(s == 1)
            def _():
                norm(m)

        lax.fori_loop(0, n + LAG, functools.partial(up_step, m), 0)
        lax.fori_loop(0, nb, functools.partial(down_step, m), 0)
    close(M - 1)

    for m in range(M):
        @pl.when(s == 0)
        def _():
            h_copy(m).wait_send()

        for d in range(1, R):
            ss_copy(m, d).wait_send()
        for d in range(1, C):
            ag_copy(m, d, c).wait_send()

        def drain_row(i, carry):
            for d in range(1, R):
                gu_copy(m, i, d).wait_send()
                hd_copy(m, i, d, r).wait_send()
            return carry

        lax.fori_loop(0, n, drain_row, 0)

        def drain_col(i, carry):
            for d in range(1, C):
                fo_copy(m, i, d).wait_send()
            return carry

        lax.fori_loop(0, nb, drain_col, 0)


def on_device(tokens, norm_gain, w_gate, w_up, w_down):
    C = lax.axis_size("col")
    R = lax.axis_size("row")
    M, TC, DR = tokens.shape
    FC = w_gate.shape[2]
    D = DR * R
    T = TC * C
    TS = T // R
    F = widest(FC, (256, 128))
    n = FC // F
    N = widest(DR, (512, 256, 128))
    nb = DR // N
    bf, f32 = jnp.bfloat16, jnp.float32
    acts = [
        ((M, TC, DR), bf),
        ((M, TC, 128), f32),
        ((M, R - 1, TC, 128), f32),
        ((M, T, DR), bf),
        ((M, n, T, 2 * F), bf),
        ((M, n, R - 1, TS, 2 * F), bf),
        ((M, T, FC), bf),
        ((M, T, DR), bf),
        ((M, C - 1, TC, DR), bf),
    ]

    def size(shape, dtype):
        total = jnp.dtype(dtype).itemsize
        for extent in shape:
            total *= extent
        return total

    used = sum(size(*a) for a in acts) + 2 * size((M, TC, DR), bf) + 8 * size((1, DR), f32)
    room = VMEM_BYTES - RESERVE - used
    a_bytes = size((2, DR, F), bf)
    b_bytes = size((FC, N), bf)
    SB = min(nb, max(2, (room // 3) // b_bytes))
    S = min(n, (room - SB * b_bytes) // a_bytes)
    dma = pltpu.SemaphoreType.DMA
    dims = (C, R, M, TC, DR, FC, D, F, n, S, N, nb, SB)
    vmem = pl.BlockSpec(memory_space=pltpu.VMEM)
    hbm = pl.BlockSpec(memory_space=pl.ANY)
    return pl.pallas_call(
        functools.partial(kernel, dims),
        out_shape=jax.ShapeDtypeStruct((1, M, TC, DR), bf),
        in_specs=[vmem, vmem, hbm, hbm, hbm],
        out_specs=vmem,
        scratch_shapes=[
            pltpu.VMEM((S, 2, DR, F), bf),
            pltpu.VMEM((SB, FC, N), bf),
            *[pltpu.VMEM(shape, dtype) for shape, dtype in acts],
            dma((S, 2)), dma((SB,)),
            dma((M,)), dma((M,)),
            dma((M, R - 1)), dma((M, R - 1)),
            dma((M, C - 1)), dma((M, C - 1)),
            dma((M, n, R - 1)), dma((M, n, R - 1)),
            dma((M, n, R - 1)), dma((M, n, R - 1)),
            dma((M, nb, C - 1)), dma((M, nb, C - 1)),
        ],
        compiler_params=pltpu.CompilerParams(
            collective_id=0, has_side_effects=True, vmem_limit_bytes=VMEM_BYTES
        ),
        name="two_blocks",
    )(tokens, norm_gain, w_gate, w_up, w_down)


def solution(mesh):
    placed = (
        P(None, ("group", "col"), "row"),
        P("section", "row"),
        P("section", "row", "col"),
        P("section", "row", "col"),
        P("section", "col", "row"),
    )
    return jax.shard_map(
        on_device,
        mesh=mesh,
        in_specs=placed,
        out_specs=P("section", None, ("group", "col"), "row"),
        check_vma=False,
    )
```
